128 devices in a mesh: mic: 8 (over x_lo, z), tm: 16 (over x_hi, y, core).
Axes of the slice: x: 4 (x_hi: 2, x_lo: 2; x = x_hi * 2 + x_lo), y: 4, z: 4, core: 2. Of those that a mesh axis runs over, the one named last changes fastest.
Arguments:
- signal: float32 [8, 16384, 512], P('mic', 'tm'), may hold values from -6 to 6
- conv_weight: float32 [2, 3, 2, 512, 512], replicated, may hold values from -0.1875 to 0.1875
- conv_bias: float32 [2, 3, 512], replicated, may hold values from -3 to 3
- transform_in: float32 [2, 512, 512], replicated, may hold values from -0.25 to 0.25
- transform_mid: float32 [2, 512, 512], replicated, may hold values from -0.25 to 0.25
- transform_out: float32 [2, 1024, 512], replicated, may hold values from -0.1875 to 0.1875
- transform_offsets_bias: float32 [2, 3, 512], replicated, may hold values from -3 to 3
Outputs:
- separated: float32 [8, 16384, 512], P('mic', 'tm')
The draws below stay inside these ranges and needn't reach their ends.
All inputs are finite; a program needn't handle non-finite values.
Results may differ from the reference program's by a relative error of at most 0.0001.
Values sent between devices are 32-bit elements; how exact they have to be, the bound alone decides.
No kernel may reach another device: no remote copies, remote signals or barrier semaphores. Data moves between devices by JAX's collectives and lax.ppermute only.
A program may use at most 128 MiB of HBM per device.

```python
import jax
import jax.numpy as jnp
from jax import lax

C = 512
SEPARATOR_BLOCKS = 2
LAYERS = 3
BASE_DILATION = 512
MICS = 8
FRAMES = 16384


def shard_levels(own_key, shape, shards, least, high):
    loudness = 1.0
    for position, parts in shards:
        heights = jax.random.uniform(jax.random.fold_in(jax.random.fold_in(own_key, 6), position), (parts,), jnp.float32, least / len(shards), high / len(shards))
        loudness = loudness * jnp.repeat(jnp.exp(heights), shape[position] // parts).reshape((-1,) + (1,) * (len(shape) - 1 - position))
    return loudness


def centred(own_key, shape, scale, bound, split=(), held_as=jnp.bfloat16):
    array = scale * jax.random.normal(own_key, shape, jnp.float32)
    if split:
        array = array * shard_levels(own_key, shape, split, -0.22, 0.18)
    return jnp.clip(array, -bound, bound).astype(held_as)


def setup_inputs(seed: int = 0) -> dict:
    key_of = jax.random.split(jax.random.key(seed), 8)
    return {
        "signal": centred(key_of[0], (MICS, FRAMES, C), 1.0, 6.0, ((0, 8), (1, 16)), jnp.float32),
        "conv_weight": centred(key_of[1], (SEPARATOR_BLOCKS, LAYERS, 2, C, C), (2 * C) ** -0.5, 0.1875, (), jnp.float32),
        "conv_bias": centred(key_of[2], (SEPARATOR_BLOCKS, LAYERS, C), 0.5, 3.0, (), jnp.float32),
        "transform_in": centred(key_of[3], (SEPARATOR_BLOCKS, C, C), C ** -0.5, 0.25, (), jnp.float32),
        "transform_mid": centred(key_of[4], (SEPARATOR_BLOCKS, C, C), C ** -0.5, 0.25, (), jnp.float32),
        "transform_out": centred(key_of[5], (SEPARATOR_BLOCKS, 2 * C, C), (2 * C) ** -0.5, 0.1875, (), jnp.float32),
        "transform_offsets_bias": centred(key_of[6], (SEPARATOR_BLOCKS, 3, C), 0.5, 3.0, (), jnp.float32),
    }


def product(left, right):
    return jnp.einsum("mtc,cd->mtd", left, right, precision=lax.Precision.HIGHEST)


def delay_frames(values, dilation_factor):
    padding_frames = jnp.zeros((values.shape[0], dilation_factor, values.shape[2]), jnp.float32)
    return jnp.concatenate([padding_frames, values[:, :values.shape[1] - dilation_factor]], axis=1)


def reference(signal, conv_weight, conv_bias, transform_in, transform_mid, transform_out, transform_offsets_bias):
    hidden_activations = signal
    for section_index in range(SEPARATOR_BLOCKS):
        for layer_position in range(LAYERS):
            dilation_factor = BASE_DILATION * 2 ** layer_position
            delayed = delay_frames(hidden_activations, dilation_factor)
            before_tanh = product(hidden_activations, conv_weight[section_index, layer_position, 0]) + product(delayed, conv_weight[section_index, layer_position, 1]) + conv_bias[section_index, layer_position]
            hidden_activations = hidden_activations + jnp.tanh(before_tanh)
        mapped = jnp.tanh(product(hidden_activations, transform_in[section_index]) + transform_offsets_bias[section_index, 0])
        channel_mean = jnp.sum(mapped, axis=0, keepdims=True) / jnp.float32(MICS)
        pooled = jnp.tanh(product(channel_mean, transform_mid[section_index]) + transform_offsets_bias[section_index, 1])
        mixing = product(mapped, transform_out[section_index, :C]) + product(pooled, transform_out[section_index, C:]) + transform_offsets_bias[section_index, 2]
        hidden_activations = hidden_activations + jnp.tanh(mixing)
    return hidden_activations
```

```python
import functools

import jax
import jax.numpy as jnp
from jax import lax
from jax.experimental import pallas as pl
from jax.experimental.pallas import tpu as pltpu
from jax.sharding import PartitionSpec as P

SECTIONS = 2
LAYERS = 3
BASE = 512
MICS = 8
LANES = 512
TILE = 8
COLS = 128
CHUNKS = 2
F32 = jnp.float32
BF16 = jnp.bfloat16
BOTH = ("mic", "tm")
VMEM = pl.BlockSpec(memory_space=pltpu.VMEM)
ANY = pl.BlockSpec(memory_space=pl.ANY)


def halves(x):
    hi = x.astype(BF16)
    lo = (x - hi.astype(F32)).astype(BF16)
    return hi, lo


def pack_kernel(chunk, x_ref, out_ref):
    rows = TILE // CHUNKS
    groups = LANES // COLS
    for k in range(rows):
        start = 128 * (chunk + CHUNKS * k)
        for g in range(groups):
            out_ref[pl.ds(g * rows + k, 128, stride=groups * rows), :] = x_ref[
                start : start + 128, g * COLS : (g + 1) * COLS
            ]


def unpack_kernel(*refs):
    y_refs, out_ref = refs[:-1], refs[-1]
    rows = TILE // CHUNKS
    groups = LANES // COLS
    for chunk, y_ref in enumerate(y_refs):
        for k in range(rows):
            start = 128 * (chunk + CHUNKS * k)
            for g in range(groups):
                out_ref[start : start + 128, g * COLS : (g + 1) * COLS] = y_ref[
                    pl.ds(g * rows + k, 128, stride=groups * rows), :
                ]


def split_kernel(*refs):
    n = len(refs) // 3
    for i in range(n):
        hi, lo = halves(refs[i][...])
        refs[n + 2 * i][...] = hi
        refs[n + 2 * i + 1][...] = lo


def split_weights(arrays):
    steps = 8
    specs = [pl.BlockSpec((a.shape[0] // steps, a.shape[1]), lambda i: (i, 0)) for a in arrays]
    size = sum(a.size for a in arrays)
    return pl.pallas_call(
        split_kernel,
        grid=(steps,),
        in_specs=specs,
        out_specs=[s for s in specs for _ in range(2)],
        out_shape=[jax.ShapeDtypeStruct(a.shape, BF16) for a in arrays for _ in range(2)],
        cost_estimate=pl.CostEstimate(flops=4 * size, bytes_accessed=8 * size, transcendentals=0),
        name="split_weights",
    )(*arrays)


def dot3(ahi, alo, whi, wlo):
    dot = functools.partial(jnp.dot, preferred_element_type=F32)
    return dot(ahi, whi) + dot(ahi, wlo) + dot(alo, whi)


def network_kernel(per, block, x_ref, cb_ref, tb_ref, *refs):
    (c_hi, c_lo, i_hi, i_lo, m_hi, m_lo, o_hi, o_lo, out_ref) = refs[:9]
    (h_ref, a_hi, a_lo, u_ref, u_hi, u_lo, p_ref) = refs[9:16]
    (wc_hi, wc_lo, wi_hi, wi_lo, wm_hi, wm_lo, wo_hi, wo_lo, sems) = refs[16:]
    rows, width = h_ref.shape
    step = per * MICS
    pad = a_hi.shape[1] - rows
    quotients = rows // step
    groups = width // COLS
    piece = 2 * per * groups

    def copies(s):
        out = []
        for l in range(LAYERS):
            k = s * LAYERS + l
            out += [(c_hi.at[k], wc_hi.at[k], sems.at[s, 2 * l]), (c_lo.at[k], wc_lo.at[k], sems.at[s, 2 * l + 1])]
        for j, (src, dst) in enumerate(
            [(i_hi, wi_hi), (i_lo, wi_lo), (m_hi, wm_hi), (m_lo, wm_lo), (o_hi, wo_hi), (o_lo, wo_lo)]
        ):
            out.append((src.at[s], dst.at[s], sems.at[s, 2 * LAYERS + j]))
        return [pltpu.make_async_copy(*c) for c in out]

    for s in range(SECTIONS):
        for c in copies(s):
            c.start()

    for slot in range(2):
        a_hi[slot, 0:pad, :] = jnp.zeros((pad, width), BF16)
        a_lo[slot, 0:pad, :] = jnp.zeros((pad, width), BF16)

    tms = x_ref.shape[0] // piece // MICS
    for tm in range(tms):
        for qp in range(2):
            for r in range(per):
                row = ((2 * tm + qp) * per + r) * MICS
                for g in range(groups):
                    h_ref[row : row + MICS, g * COLS : (g + 1) * COLS] = x_ref[
                        pl.ds(tm * piece + (g * 2 + qp) * per + r, MICS, stride=tms * piece), :
                    ]

    blocks = rows // block

    def put(slot, start, h):
        hi, lo = halves(h)
        a_hi[slot, pl.ds(pad + start, block), :] = hi
        a_lo[slot, pl.ds(pad + start, block), :] = lo

    def first(b, _):
        start = pl.multiple_of(b * block, block)
        put(0, start, h_ref[pl.ds(start, block), :])
        return 0

    lax.fori_loop(0, blocks, first, 0)

    def section(s, _):
        def layer(l, _):
            k = s * LAYERS + l
            cur = lax.rem(l, 2)
            shift = pl.multiple_of(step * lax.shift_left(1, l), step)
            pltpu.make_async_copy(c_hi.at[k], wc_hi.at[k], sems.at[s, 2 * l]).wait()
            pltpu.make_async_copy(c_lo.at[k], wc_lo.at[k], sems.at[s, 2 * l + 1]).wait()

            def one(b, _):
                start = pl.multiple_of(b * block, block)
                here = pl.ds(pad + start, block)
                past = pl.ds(pl.multiple_of(pad + start - shift, step), block)
                pre = dot3(a_hi[cur, here, :], a_lo[cur, here, :], wc_hi[k, :width, :], wc_lo[k, :width, :])
                pre += dot3(a_hi[cur, past, :], a_lo[cur, past, :], wc_hi[k, width:, :], wc_lo[k, width:, :])
                h = h_ref[pl.ds(start, block), :] + jnp.tanh(pre + cb_ref[pl.ds(k, 1), :])
                h_ref[pl.ds(start, block), :] = h
                put(1 - cur, start, h)
                return 0

            lax.fori_loop(0, blocks, one, 0)
            return 0

        lax.fori_loop(0, LAYERS, layer, 0)
        last = LAYERS % 2
        for j, (src, dst) in enumerate(
            [(i_hi, wi_hi), (i_lo, wi_lo), (m_hi, wm_hi), (m_lo, wm_lo), (o_hi, wo_hi), (o_lo, wo_lo)]
        ):
            pltpu.make_async_copy(src.at[s], dst.at[s], sems.at[s, 2 * LAYERS + j]).wait()

        def inner(b, _):
            start = pl.multiple_of(b * block, block)
            here = pl.ds(pad + start, block)
            pre = dot3(a_hi[last, here, :], a_lo[last, here, :], wi_hi[s], wi_lo[s])
            u = jnp.tanh(pre + tb_ref[pl.ds(3 * s, 1), :])
            for g in range(groups):
                u_ref[g, pl.ds(start, block), :] = u[:, g * COLS : (g + 1) * COLS]
            hi, lo = halves(u)
            u_hi[pl.ds(start, block), :] = hi
            u_lo[pl.ds(start, block), :] = lo
            return 0

        lax.fori_loop(0, blocks, inner, 0)

        frames = rows // MICS
        means = []
        for g in range(groups):
            total = u_ref[g, pl.ds(0, frames, stride=MICS), :]
            for m in range(1, MICS):
                total += u_ref[g, pl.ds(m, frames, stride=MICS), :]
            means.append(total * (1.0 / MICS))
        hi, lo = halves(jnp.concatenate(means, axis=1))
        v = jnp.tanh(dot3(hi, lo, wm_hi[s], wm_lo[s]) + tb_ref[pl.ds(3 * s + 1, 1), :])
        hi, lo = halves(v)
        p_ref[...] = dot3(hi, lo, wo_hi[s, width:, :], wo_lo[s, width:, :]) + tb_ref[pl.ds(3 * s + 2, 1), :]

        def outer(b, _):
            start = pl.multiple_of(b * block, block)
            here = pl.ds(start, block)
            pre = dot3(u_hi[here, :], u_lo[here, :], wo_hi[s, :width, :], wo_lo[s, :width, :])
            base = pl.multiple_of(b * (block // MICS), block // MICS)
            pooled = jnp.concatenate(
                [jnp.broadcast_to(p_ref[pl.ds(base + j, 1), :], (MICS, width)) for j in range(block // MICS)], axis=0
            )
            h = h_ref[here, :] + jnp.tanh(pre + pooled)
            h_ref[here, :] = h
            put(0, start, h)
            return 0

        lax.fori_loop(0, blocks, outer, 0)
        return 0

    lax.fori_loop(0, SECTIONS, section, 0)

    for tm in range(tms):
        for qp in range(2):
            for r in range(per):
                row = ((2 * tm + qp) * per + r) * MICS
                for g in range(groups):
                    out_ref[pl.ds(tm * piece + (g * 2 + qp) * per + r, MICS, stride=tms * piece), :] = h_ref[
                        row : row + MICS, g * COLS : (g + 1) * COLS
                    ]


def network(x, biases, weights, block=256):
    rows = x.size // LANES
    width = LANES
    per = rows // MICS // 32
    pad = 4 * per * MICS
    cb, tb = biases
    scratch = [
        pltpu.VMEM((rows, width), F32),
        pltpu.VMEM((2, pad + rows, width), BF16),
        pltpu.VMEM((2, pad + rows, width), BF16),
        pltpu.VMEM((width // COLS, rows, COLS), F32),
        pltpu.VMEM((rows, width), BF16),
        pltpu.VMEM((rows, width), BF16),
        pltpu.VMEM((rows // MICS, width), F32),
    ]
    scratch += [pltpu.VMEM(w.shape, BF16) for w in weights]
    scratch += [pltpu.SemaphoreType.DMA((SECTIONS, 2 * LAYERS + 6))]
    flops = 2 * 3 * rows * width * width * (SECTIONS * (2 * LAYERS + 2)) + 2 * 3 * rows // MICS * width * width * 4
    return pl.pallas_call(
        functools.partial(network_kernel, per, block),
        in_specs=[VMEM] * 3 + [ANY] * len(weights),
        out_specs=VMEM,
        out_shape=jax.ShapeDtypeStruct(x.shape, F32),
        scratch_shapes=scratch,
        compiler_params=pltpu.CompilerParams(vmem_limit_bytes=48 << 20),
        cost_estimate=pl.CostEstimate(
            flops=flops, bytes_accessed=sum(2 * w.size for w in weights), transcendentals=rows * width * 10
        ),
        name="network",
    )(x, cb, tb, *weights)


def pack(x, chunk):
    return pl.pallas_call(
        functools.partial(pack_kernel, chunk),
        in_specs=[VMEM],
        out_specs=VMEM,
        out_shape=jax.ShapeDtypeStruct((x.size // CHUNKS // COLS, COLS), F32),
        name="pack",
    )(x)


def exchange(x):
    devices = lax.axis_size(BOTH)
    pieces = x.reshape(devices, x.shape[0] // devices, x.shape[1])
    return lax.all_to_all(pieces, BOTH, 0, 0, tiled=True).reshape(x.shape)


def body(signal, conv_weight, conv_bias, transform_in, transform_mid, transform_out, transform_offsets_bias):
    x = signal[0]
    width = x.shape[1]
    received = [exchange(pack(x, c)) for c in range(CHUNKS)]
    flat = [w.reshape(-1, width) for w in (conv_weight, transform_in, transform_mid, transform_out)]
    c_hi, c_lo, i_hi, i_lo, m_hi, m_lo, o_hi, o_lo = split_weights(flat)
    weights = [w.reshape(SECTIONS * LAYERS, 2 * width, width) for w in (c_hi, c_lo)]
    weights += [w.reshape(SECTIONS, width, width) for w in (i_hi, i_lo, m_hi, m_lo)]
    weights += [w.reshape(SECTIONS, 2 * width, width) for w in (o_hi, o_lo)]
    biases = conv_bias.reshape(-1, width), transform_offsets_bias.reshape(-1, width)
    back = [exchange(network(y, biases, weights)) for y in received]
    return pl.pallas_call(
        unpack_kernel,
        in_specs=[VMEM] * CHUNKS,
        out_specs=VMEM,
        out_shape=jax.ShapeDtypeStruct(x.shape, F32),
        name="unpack",
    )(*back)[None]


def solution(mesh):
    placed = (P("mic", "tm", None), P(), P(), P(), P(), P(), P())
    return jax.shard_map(body, mesh=mesh, in_specs=placed, out_specs=P("mic", "tm", None), check_vma=False)
```

```python
import functools

import jax
import jax.numpy as jnp
from jax import lax
from jax.experimental import pallas as pl
from jax.experimental.pallas import tpu as pltpu
from jax.sharding import PartitionSpec as P

SECTIONS = 2
LAYERS = 3
MICS = 8
COLS = 128
GRANT = 65400 * 1024
F32 = jnp.float32
BF16 = jnp.bfloat16
BOTH = ("mic", "tm")
VMEM = pl.BlockSpec(memory_space=pltpu.VMEM)
ANY = pl.BlockSpec(memory_space=pl.ANY)
PARAMS = pltpu.CompilerParams(vmem_limit_bytes=GRANT)


def halves(x):
    hi = x.astype(BF16)
    lo = (x - hi.astype(F32)).astype(BF16)
    return hi, lo


def taps_kernel(w_ref, hi_ref, lo_ref):
    width = w_ref.shape[1]
    now, past = w_ref[:width, :], w_ref[width:, :]
    for i, w in enumerate((now, past, now + past)):
        part = slice(i * width, (i + 1) * width)
        hi_ref[part, :], lo_ref[part, :] = halves(w)


def split_taps(w):
    layers = SECTIONS * LAYERS
    rows, width = w.shape
    spec = pl.BlockSpec((rows // layers // 2 * 3, width), lambda i: (i, 0))
    out = jax.ShapeDtypeStruct((rows // 2 * 3, width), BF16)
    return pl.pallas_call(
        taps_kernel,
        grid=(layers,),
        in_specs=[pl.BlockSpec((rows // layers, width), lambda i: (i, 0))],
        out_specs=[spec] * 2,
        out_shape=[out] * 2,
        compiler_params=PARAMS,
        cost_estimate=pl.CostEstimate(flops=6 * w.size, bytes_accessed=10 * w.size, transcendentals=0),
        name="split_taps",
    )(w)


def dense_kernel(*refs):
    n = len(refs) // 3
    for i in range(n):
        refs[n + 2 * i][...], refs[n + 2 * i + 1][...] = halves(refs[i][...])


def split_dense(arrays, steps=4):
    specs = [pl.BlockSpec((a.shape[0] // steps, a.shape[1]), lambda i: (i, 0)) for a in arrays]
    size = sum(a.size for a in arrays)
    return pl.pallas_call(
        dense_kernel,
        grid=(steps,),
        in_specs=specs,
        out_specs=[p for p in specs for _ in range(2)],
        out_shape=[jax.ShapeDtypeStruct(a.shape, BF16) for a in arrays for _ in range(2)],
        compiler_params=PARAMS,
        cost_estimate=pl.CostEstimate(flops=4 * size, bytes_accessed=8 * size, transcendentals=0),
        name="split_dense",
    )(*arrays)


def dot3(a, w):
    dot = functools.partial(jnp.dot, preferred_element_type=F32)
    return dot(a[0], w[0]) + dot(a[0], w[1]) + dot(a[1], w[0])


def network_kernel(per, x_ref, cb_ref, tb_ref, *refs):
    n = 8
    sources, out_ref, h_ref, u_ref = refs[:n], *refs[n : n + 3]
    held, sems = refs[n + 3 : 2 * n + 3], refs[2 * n + 3]
    rows, width = h_ref.shape
    step = per * MICS
    groups = width // COLS
    piece = 2 * per * groups
    tms = x_ref.shape[0] // piece // MICS

    def fetch(j, k):
        size = held[j].shape[0] // (SECTIONS * LAYERS if j < 2 else SECTIONS)
        part = pl.ds(pl.multiple_of(k * size, size), size)
        return pltpu.make_async_copy(sources[j].at[part, :], held[j].at[part, :], sems.at[j, k])

    for s in range(SECTIONS):
        for l in range(LAYERS):
            for j in range(2):
                fetch(j, s * LAYERS + l).start()
        for j in range(2, n):
            fetch(j, s).start()

    def spots():
        for tm in range(tms):
            for qp in range(2):
                for r in range(per):
                    row = ((2 * tm + qp) * per + r) * MICS
                    for g in range(groups):
                        spot = pl.ds(tm * piece + (g * 2 + qp) * per + r, MICS, stride=tms * piece)
                        yield spot, slice(row, row + MICS), slice(g * COLS, (g + 1) * COLS)

    def weight(j, first):
        part = pl.ds(pl.multiple_of(first, width), width)
        return held[j][part, :], held[j + 1][part, :]

    def layer(s, l):
        k = s * LAYERS + l
        for j in range(2):
            fetch(j, k).wait()
        span = step * 2**l
        evens = [pl.ds(2 * p * span, span) for p in range(rows // span // 2)]
        odds = [pl.ds((2 * p + 1) * span, span) for p in range(rows // span // 2)]
        even = jnp.concatenate([h_ref[p, :] for p in evens], axis=0)
        odd = jnp.concatenate([h_ref[p, :] for p in odds], axis=0)
        past = jnp.concatenate([jnp.zeros((span, width), F32)] + [h_ref[p, :] for p in odds[:-1]], axis=0)
        first = 3 * k * width
        shared = dot3(halves(even), weight(0, first + 2 * width)) + cb_ref[s, l : l + 1, :]
        y_even = shared + dot3(halves(past - even), weight(0, first + width))
        y_odd = shared + dot3(halves(odd - even), weight(0, first))
        for where, y in ((evens, y_even), (odds, y_odd)):
            for i, p in enumerate(where):
                h_ref[p, :] = h_ref[p, :] + jnp.tanh(y[i * span : (i + 1) * span])

    for spot, row, lane in spots():
        h_ref[row, lane] = x_ref[spot, :]
    layer(0, 0)

    def section(s, _):
        for l in range(1, LAYERS):
            layer(s, l)
        for j in range(2, n):
            fetch(j, s).wait()
        u = jnp.tanh(dot3(halves(h_ref[...]), weight(2, s * width)) + tb_ref[s, 0:1, :])
        for g in range(groups):
            u_ref[g, :, :] = u[:, g * COLS : (g + 1) * COLS]
        mixed = dot3(halves(u), weight(6, 2 * s * width))

        frames = rows // MICS
        means = []
        for g in range(groups):
            total = u_ref[g, pl.ds(0, frames, stride=MICS), :]
            for m in range(1, MICS):
                total += u_ref[g, pl.ds(m, frames, stride=MICS), :]
            means.append(total * (1.0 / MICS))
        mean = jnp.concatenate(means, axis=1)
        v = jnp.tanh(dot3(halves(mean), weight(4, s * width)) + tb_ref[s, 1:2, :])
        pooled = dot3(halves(v), weight(6, 2 * s * width + width)) + tb_ref[s, 2:3, :]
        pooled = jnp.broadcast_to(pooled[:, None, :], (frames, MICS, width)).reshape(rows, width)
        h = h_ref[...] + jnp.tanh(mixed + pooled)
        h_ref[...] = h
        for spot, row, lane in spots():
            out_ref[spot, :] = h[row, lane]

        @pl.when(s < SECTIONS - 1)
        def _():
            layer(s + 1, 0)

        return 0

    lax.fori_loop(0, SECTIONS, section, 0)


def network(x, biases, weights):
    width = weights[0].shape[1]
    rows = x.size // width
    per = rows // MICS // 32
    scratch = [pltpu.VMEM((rows, width), F32), pltpu.VMEM((width // COLS, rows, COLS), F32)]
    scratch += [pltpu.VMEM(w.shape, w.dtype) for w in weights]
    scratch += [pltpu.SemaphoreType.DMA((len(weights), SECTIONS * LAYERS))]
    flops = 6 * rows * width * width * SECTIONS * (3 * LAYERS // 2 + 2)
    return pl.pallas_call(
        functools.partial(network_kernel, per),
        in_specs=[VMEM] * 3 + [ANY] * len(weights),
        out_specs=VMEM,
        out_shape=jax.ShapeDtypeStruct(x.shape, F32),
        scratch_shapes=scratch,
        compiler_params=PARAMS,
        cost_estimate=pl.CostEstimate(
            flops=flops, bytes_accessed=8 * x.size + sum(w.nbytes for w in weights), transcendentals=rows * width * 10
        ),
        name="network",
    )(x, *biases, *weights)


def exchange(pieces):
    return lax.all_to_all(pieces, BOTH, 0, 0, tiled=True)


def body(signal, conv_weight, conv_bias, transform_in, transform_mid, transform_out, transform_offsets_bias):
    frames, width = signal.shape[1:]
    devices = lax.axis_size(BOTH)
    held = frames // devices
    groups = width // COLS
    pieces = signal.reshape(held, devices, width).transpose(1, 0, 2)
    pieces = exchange(pieces)
    x = pieces.reshape(devices, held, groups, COLS).transpose(0, 2, 1, 3).reshape(-1, COLS)
    flat = [w.reshape(-1, width) for w in (transform_in, transform_mid, transform_out)]
    weights = [*split_taps(conv_weight.reshape(-1, width)), *split_dense(flat)]
    y = network(x, (conv_bias, transform_offsets_bias), weights)
    pieces = y.reshape(devices, groups, held, COLS).transpose(0, 2, 1, 3).reshape(devices, held, width)
    pieces = exchange(pieces)
    return pieces.transpose(1, 0, 2).reshape(signal.shape)


def solution(mesh):
    placed = (P("mic", "tm", None), P(), P(), P(), P(), P(), P())
    return jax.shard_map(body, mesh=mesh, in_specs=placed, out_specs=P("mic", "tm", None), check_vma=False)
```

```python
import functools

import jax
import jax.numpy as jnp
from jax import lax
from jax.experimental import pallas as pl
from jax.experimental.pallas import tpu as pltpu
from jax.sharding import PartitionSpec as P

SECTIONS = 2
LAYERS = 3
MICS = 8
TILE = 8
GRANT = 65400 * 1024
F32 = jnp.float32
BF16 = jnp.bfloat16
BOTH = ("mic", "tm")
VMEM = pl.BlockSpec(memory_space=pltpu.VMEM)
ANY = pl.BlockSpec(memory_space=pl.ANY)
PARAMS = pltpu.CompilerParams(vmem_limit_bytes=GRANT)


def halves(x):
    hi = x.astype(BF16)
    lo = (x - hi.astype(F32)).astype(BF16)
    return hi, lo


def taps_kernel(w_ref, hi_ref, lo_ref):
    width = w_ref.shape[1]
    now, past = w_ref[:width, :], w_ref[width:, :]
    for i, w in enumerate((now + past, now, past)):
        part = slice(i * width, (i + 1) * width)
        hi_ref[part, :], lo_ref[part, :] = halves(w)


def split_taps(w):
    layers = SECTIONS * LAYERS
    rows, width = w.shape
    spec = pl.BlockSpec((rows // layers // 2 * 3, width), lambda i: (i, 0))
    out = jax.ShapeDtypeStruct((rows // 2 * 3, width), BF16)
    return pl.pallas_call(
        taps_kernel,
        grid=(layers,),
        in_specs=[pl.BlockSpec((rows // layers, width), lambda i: (i, 0))],
        out_specs=[spec] * 2,
        out_shape=[out] * 2,
        compiler_params=PARAMS,
        cost_estimate=pl.CostEstimate(flops=6 * w.size, bytes_accessed=10 * w.size, transcendentals=0),
        name="split_taps",
    )(w)


def dense_kernel(*refs):
    n = len(refs) // 3
    for i in range(n):
        refs[n + 2 * i][...], refs[n + 2 * i + 1][...] = halves(refs[i][...])


def split_dense(arrays, steps=4):
    specs = [pl.BlockSpec((a.shape[0] // steps, a.shape[1]), lambda i: (i, 0)) for a in arrays]
    size = sum(a.size for a in arrays)
    return pl.pallas_call(
        dense_kernel,
        grid=(steps,),
        in_specs=specs,
        out_specs=[p for p in specs for _ in range(2)],
        out_shape=[jax.ShapeDtypeStruct(a.shape, BF16) for a in arrays for _ in range(2)],
        compiler_params=PARAMS,
        cost_estimate=pl.CostEstimate(flops=4 * size, bytes_accessed=8 * size, transcendentals=0),
        name="split_dense",
    )(*arrays)


def dot3(a, w):
    dot = functools.partial(jnp.dot, preferred_element_type=F32)
    return dot(a[0], w[0]) + dot(a[0], w[1]) + dot(a[1], w[0])


def network_kernel(x_ref, cb_ref, tb_ref, *refs):
    n = 8
    sources, h_ref = refs[:n], refs[n]
    held, sems = refs[n + 1 : 2 * n + 1], refs[2 * n + 1]
    rows, width = h_ref.shape
    frames = rows // MICS
    half = TILE // 2

    def fetch(j, k):
        size = width if j < 2 else held[j].shape[0] // SECTIONS
        part = pl.ds(pl.multiple_of(k * size, size), size)
        return pltpu.make_async_copy(sources[j].at[part, :], held[j].at[part, :], sems.at[j, k])

    for s in range(SECTIONS):
        for k in range(3 * LAYERS * s, 3 * LAYERS * (s + 1)):
            for j in range(2):
                fetch(j, k).start()
        for j in range(2, n):
            fetch(j, s).start()

    def weight(j, k):
        part = pl.ds(pl.multiple_of(k * width, width), width)
        return held[j][part, :], held[j + 1][part, :]

    top = lax.broadcasted_iota(jnp.int32, (rows // TILE // 2, TILE, width), 1) < half

    def swap(a):
        return pltpu.roll(a, half, axis=1)

    def pair(h, l):
        if l == 0:
            tiles = h.reshape(rows // TILE // 2, 2, TILE, width)
            a, b = tiles[:, 0], tiles[:, 1]
            even, odd = jnp.where(top, a, swap(b)), jnp.where(top, swap(a), b)
            turned = swap(odd).reshape(MICS, -1, TILE, width)
            before = jnp.concatenate([jnp.zeros((MICS, 1, TILE, width), F32), turned[:, :-1]], axis=1)
            past = jnp.where(top, before.reshape(odd.shape), turned.reshape(odd.shape))
        else:
            groups = h.reshape(MICS, -1, 2, half * 2**l, width)
            even, odd = groups[:, :, 0], groups[:, :, 1]
            past = jnp.concatenate([jnp.zeros_like(odd[:, :1]), odd[:, :-1]], axis=1)
        return [p.reshape(rows // 2, width) for p in (even, odd, past)]

    def join(even, odd, l):
        if l == 0:
            even, odd = (p.reshape(rows // TILE // 2, 1, TILE, width) for p in (even, odd))
            even, odd = even[:, 0], odd[:, 0]
            a, b = jnp.where(top, even, swap(odd)), jnp.where(top, swap(even), odd)
            both = jnp.concatenate([a[:, None], b[:, None]], axis=1)
        else:
            even, odd = (p.reshape(MICS, -1, 1, half * 2**l, width) for p in (even, odd))
            both = jnp.concatenate([even, odd], axis=2)
        return both.reshape(rows, width)

    def layer(h, s, l, eager):
        k = 3 * (s * LAYERS + l)

        def ready(*taps):
            for t in taps:
                for j in range(2):
                    fetch(j, k + t).wait()

        if not eager:
            ready(0, 1, 2)
        even, odd, past = pair(h, l)
        if eager:
            ready(0)
        shared = dot3(halves(even), weight(0, k)) + cb_ref[s, l : l + 1, :]
        if eager:
            ready(1, 2)
        y_odd = shared + dot3(halves(odd - even), weight(0, k + 1))
        y_even = shared + dot3(halves(past - even), weight(0, k + 2))
        h_ref[...] = join(even + jnp.tanh(y_even), odd + jnp.tanh(y_odd), l)

    layer(x_ref[...], 0, 0, True)

    def section(s, _):
        for l in range(1, LAYERS):
            layer(h_ref[...], s, l, False)
        for j in range(2, n):
            fetch(j, s).wait()
        u = jnp.tanh(dot3(halves(h_ref[...]), weight(2, s)) + tb_ref[s, 0:1, :])
        total = u[:frames]
        for m in range(1, MICS):
            total += u[m * frames : (m + 1) * frames]
        v = jnp.tanh(dot3(halves(total * (1.0 / MICS)), weight(4, s)) + tb_ref[s, 1:2, :])
        pooled = dot3(halves(v), weight(6, 2 * s + 1)) + tb_ref[s, 2:3, :]
        mixed = dot3(halves(u), weight(6, 2 * s))
        for m in range(MICS):
            part = slice(m * frames, (m + 1) * frames)
            h_ref[part, :] = h_ref[part, :] + jnp.tanh(mixed[part] + pooled)

        @pl.when(s < SECTIONS - 1)
        def _():
            layer(h_ref[...], s + 1, 0, False)

        return 0

    lax.fori_loop(0, SECTIONS, section, 0)


def network(x, biases, weights):
    rows, width = x.shape
    scratch = [pltpu.VMEM(w.shape, w.dtype) for w in weights]
    scratch += [pltpu.SemaphoreType.DMA((len(weights), 3 * SECTIONS * LAYERS))]
    flops = 6 * rows * width * width * SECTIONS * (3 * LAYERS // 2 + 2)
    return pl.pallas_call(
        network_kernel,
        in_specs=[VMEM] * 3 + [ANY] * len(weights),
        out_specs=VMEM,
        out_shape=jax.ShapeDtypeStruct(x.shape, F32),
        scratch_shapes=scratch,
        compiler_params=PARAMS,
        cost_estimate=pl.CostEstimate(
            flops=flops, bytes_accessed=8 * x.size + sum(w.nbytes for w in weights), transcendentals=rows * width * 10
        ),
        name="network",
    )(x, *biases, *weights)


def exchange(pieces):
    return lax.all_to_all(pieces, BOTH, 0, 0, tiled=True)


def body(signal, conv_weight, conv_bias, transform_in, transform_mid, transform_out, transform_offsets_bias):
    frames, width = signal.shape[1:]
    devices = lax.axis_size(BOTH)
    held = frames // devices
    pieces = signal.reshape(held, devices, width).transpose(1, 0, 2)
    pieces = exchange(pieces)
    flat = [w.reshape(-1, width) for w in (transform_in, transform_mid, transform_out)]
    weights = [*split_taps(conv_weight.reshape(-1, width)), *split_dense(flat)]
    y = network(pieces.reshape(frames, width), (conv_bias, transform_offsets_bias), weights)
    pieces = exchange(y.reshape(devices, held, width))
    return pieces.transpose(1, 0, 2).reshape(signal.shape)


def solution(mesh):
    placed = (P("mic", "tm", None), P(), P(), P(), P(), P(), P())
    return jax.shard_map(body, mesh=mesh, in_specs=placed, out_specs=P("mic", "tm", None), check_vma=False)
```

```python
import functools

import jax
import jax.numpy as jnp
from jax import lax
from jax.experimental import pallas as pl
from jax.experimental.pallas import tpu as pltpu
from jax.sharding import PartitionSpec as P

SECTIONS = 2
LAYERS = 3
MICS = 8
TILE = 8
GRANT = 59500 * 1024
F32 = jnp.float32
BF16 = jnp.bfloat16
BOTH = ("mic", "tm")
VMEM = pl.BlockSpec(memory_space=pltpu.VMEM)
ANY = pl.BlockSpec(memory_space=pl.ANY)
PARAMS = pltpu.CompilerParams(vmem_limit_bytes=GRANT)


def halves(x):
    hi = x.astype(BF16)
    lo = (x - hi.astype(F32)).astype(BF16)
    return hi, lo


def taps_kernel(w_ref, hi_ref, lo_ref):
    width = w_ref.shape[1]
    now, past = w_ref[:width, :], w_ref[width:, :]
    for i, w in enumerate((now + past, now, past)):
        part = slice(i * width, (i + 1) * width)
        hi_ref[part, :], lo_ref[part, :] = halves(w)


def split_taps(w):
    layers = SECTIONS * LAYERS
    rows, width = w.shape
    spec = pl.BlockSpec((rows // layers // 2 * 3, width), lambda i: (i, 0))
    out = jax.ShapeDtypeStruct((rows // 2 * 3, width), BF16)
    return pl.pallas_call(
        taps_kernel,
        grid=(layers,),
        in_specs=[pl.BlockSpec((rows // layers, width), lambda i: (i, 0))],
        out_specs=[spec] * 2,
        out_shape=[out] * 2,
        compiler_params=PARAMS,
        cost_estimate=pl.CostEstimate(flops=6 * w.size, bytes_accessed=10 * w.size, transcendentals=0),
        name="split_taps",
    )(w)


def dense_kernel(in_ref, mid_ref, out_ref, hi_ref, lo_ref):
    first = 0
    for ref in (in_ref, mid_ref, out_ref):
        part = slice(first, first + ref.shape[0])
        hi_ref[part, :], lo_ref[part, :] = halves(ref[...])
        first += ref.shape[0]


def split_dense(arrays, parts=2):
    width = arrays[0].shape[1]
    heights = [a.shape[0] // SECTIONS for a in arrays]
    specs = [pl.BlockSpec((h, width // parts), lambda s, c: (s, c)) for h in heights + [sum(heights)] * 2]
    size = sum(a.size for a in arrays)
    return pl.pallas_call(
        dense_kernel,
        grid=(SECTIONS, parts),
        in_specs=specs[:-2],
        out_specs=specs[-2:],
        out_shape=[jax.ShapeDtypeStruct((SECTIONS * sum(heights), width), BF16)] * 2,
        compiler_params=PARAMS,
        cost_estimate=pl.CostEstimate(flops=4 * size, bytes_accessed=8 * size, transcendentals=0),
        name="split_dense",
    )(*arrays)


def dot3(a, w):
    dot = functools.partial(jnp.dot, preferred_element_type=F32)
    return dot(a[0], w[0]) + dot(a[0], w[1]) + dot(a[1], w[0])


def network_kernel(x_ref, cb_ref, tb_ref, *refs):
    n = 4
    sources, h_ref = refs[:n], refs[n]
    held, sems = refs[n + 1 : 2 * n + 1], refs[2 * n + 1]
    rows, width = h_ref.shape
    frames = rows // MICS
    half = TILE // 2

    def fetch(j, k):
        size = width if j < 2 else held[j].shape[0] // SECTIONS
        part = pl.ds(pl.multiple_of(k * size, size), size)
        return pltpu.make_async_copy(sources[j].at[part, :], held[j].at[part, :], sems.at[j, k])

    for s in range(SECTIONS):
        for k in range(3 * LAYERS * s, 3 * LAYERS * (s + 1)):
            for j in range(2):
                fetch(j, k).start()
        for j in range(2, n):
            fetch(j, s).start()

    def weight(j, k):
        part = pl.ds(pl.multiple_of(k * width, width), width)
        return held[j][part, :], held[j + 1][part, :]

    top = lax.broadcasted_iota(jnp.int32, (rows // TILE // 2, TILE, width), 1) < half

    def swap(a):
        return pltpu.roll(a, half, axis=1)

    def pair(h, l):
        if l == 0:
            tiles = h.reshape(rows // TILE // 2, 2, TILE, width)
            a, b = tiles[:, 0], tiles[:, 1]
            even, odd = jnp.where(top, a, swap(b)), jnp.where(top, swap(a), b)
            turned = swap(odd).reshape(MICS, -1, TILE, width)
            before = jnp.concatenate([jnp.zeros((MICS, 1, TILE, width), F32), turned[:, :-1]], axis=1)
            past = jnp.where(top, before.reshape(odd.shape), turned.reshape(odd.shape))
        else:
            groups = h.reshape(MICS, -1, 2, half * 2**l, width)
            even, odd = groups[:, :, 0], groups[:, :, 1]
            past = jnp.concatenate([jnp.zeros_like(odd[:, :1]), odd[:, :-1]], axis=1)
        return [p.reshape(rows // 2, width) for p in (even, odd, past)]

    def join(even, odd, l):
        if l == 0:
            even, odd = (p.reshape(rows // TILE // 2, 1, TILE, width) for p in (even, odd))
            even, odd = even[:, 0], odd[:, 0]
            a, b = jnp.where(top, even, swap(odd)), jnp.where(top, swap(even), odd)
            both = jnp.concatenate([a[:, None], b[:, None]], axis=1)
        else:
            even, odd = (p.reshape(MICS, -1, 1, half * 2**l, width) for p in (even, odd))
            both = jnp.concatenate([even, odd], axis=2)
        return both.reshape(rows, width)

    def layer(h, s, l, eager):
        k = 3 * (s * LAYERS + l)

        def ready(*taps):
            for t in taps:
                for j in range(2):
                    fetch(j, k + t).wait()

        if not eager:
            ready(0, 1, 2)
        even, odd, past = pair(h, l)
        if eager:
            ready(0)
        shared = dot3(halves(even), weight(0, k)) + cb_ref[s, l : l + 1, :]
        if eager:
            ready(1, 2)
        y_odd = shared + dot3(halves(odd - even), weight(0, k + 1))
        y_even = shared + dot3(halves(past - even), weight(0, k + 2))
        h_ref[...] = join(even + jnp.tanh(y_even), odd + jnp.tanh(y_odd), l)

    layer(x_ref[...], 0, 0, True)

    def section(s, _):
        for l in range(1, LAYERS):
            layer(h_ref[...], s, l, False)
        for j in range(2, n):
            fetch(j, s).wait()
        u = jnp.tanh(dot3(halves(h_ref[...]), weight(2, 4 * s)) + tb_ref[s, 0:1, :])
        total = u[:frames]
        for m in range(1, MICS):
            total += u[m * frames : (m + 1) * frames]
        v = jnp.tanh(dot3(halves(total * (1.0 / MICS)), weight(2, 4 * s + 1)) + tb_ref[s, 1:2, :])
        pooled = dot3(halves(v), weight(2, 4 * s + 3)) + tb_ref[s, 2:3, :]
        mixed = dot3(halves(u), weight(2, 4 * s + 2))
        for m in range(MICS):
            part = slice(m * frames, (m + 1) * frames)
            h_ref[part, :] = h_ref[part, :] + jnp.tanh(mixed[part] + pooled)

        @pl.when(s < SECTIONS - 1)
        def _():
            layer(h_ref[...], s + 1, 0, False)

        return 0

    lax.fori_loop(0, SECTIONS, section, 0)


def network(x, biases, weights):
    rows, width = x.shape
    scratch = [pltpu.VMEM(w.shape, w.dtype) for w in weights]
    scratch += [pltpu.SemaphoreType.DMA((len(weights), 3 * SECTIONS * LAYERS))]
    flops = 6 * rows * width * width * SECTIONS * (3 * LAYERS // 2 + 2)
    return pl.pallas_call(
        network_kernel,
        in_specs=[VMEM] * 3 + [ANY] * len(weights),
        out_specs=VMEM,
        out_shape=jax.ShapeDtypeStruct(x.shape, F32),
        scratch_shapes=scratch,
        compiler_params=pltpu.CompilerParams(vmem_limit_bytes=48 << 20),
        cost_estimate=pl.CostEstimate(
            flops=flops, bytes_accessed=8 * x.size + sum(w.nbytes for w in weights), transcendentals=rows * width * 10
        ),
        name="network",
    )(x, *biases, *weights)


def exchange(pieces):
    return lax.all_to_all(pieces, BOTH, 0, 0, tiled=True)


def body(signal, conv_weight, conv_bias, transform_in, transform_mid, transform_out, transform_offsets_bias):
    frames, width = signal.shape[1:]
    devices = lax.axis_size(BOTH)
    held = frames // devices
    pieces = signal.reshape(held, devices, width).transpose(1, 0, 2)
    pieces = exchange(pieces)
    flat = [w.reshape(-1, width) for w in (transform_in, transform_mid, transform_out)]
    weights = [*split_taps(conv_weight.reshape(-1, width)), *split_dense(flat)]
    y = network(pieces.reshape(frames, width), (conv_bias, transform_offsets_bias), weights)
    pieces = exchange(y.reshape(devices, held, width))
    return pieces.transpose(1, 0, 2).reshape(signal.shape)


def solution(mesh):
    placed = (P("mic", "tm", None), P(), P(), P(), P(), P(), P())
    return jax.shard_map(body, mesh=mesh, in_specs=placed, out_specs=P("mic", "tm", None), check_vma=False)
```

```python
import functools

import jax
import jax.numpy as jnp
from jax import lax
from jax.experimental import pallas as pl
from jax.experimental.pallas import tpu as pltpu
from jax.sharding import PartitionSpec as P

SECTIONS = 2
LAYERS = 3
MICS = 8
TILE = 8
GRANT = 59500 * 1024
F32 = jnp.float32
BF16 = jnp.bfloat16
BOTH = ("mic", "tm")
VMEM = pl.BlockSpec(memory_space=pltpu.VMEM)
ANY = pl.BlockSpec(memory_space=pl.ANY)
PARAMS = pltpu.CompilerParams(vmem_limit_bytes=GRANT)


def halves(x):
    hi = x.astype(BF16)
    lo = (x - hi.astype(F32)).astype(BF16)
    return hi, lo


def taps_kernel(w_ref, hi_ref, lo_ref):
    width = w_ref.shape[1]
    now, past = w_ref[:width, :], w_ref[width:, :]
    for i, w in enumerate((now + past, now, past)):
        part = slice(i * width, (i + 1) * width)
        hi_ref[part, :], lo_ref[part, :] = halves(w)


def split_taps(w):
    layers = SECTIONS * LAYERS
    rows, width = w.shape
    spec = pl.BlockSpec((rows // layers // 2 * 3, width), lambda i: (i, 0))
    out = jax.ShapeDtypeStruct((rows // 2 * 3, width), BF16)
    return pl.pallas_call(
        taps_kernel,
        grid=(layers,),
        in_specs=[pl.BlockSpec((rows // layers, width), lambda i: (i, 0))],
        out_specs=[spec] * 2,
        out_shape=[out] * 2,
        compiler_params=PARAMS,
        cost_estimate=pl.CostEstimate(flops=6 * w.size, bytes_accessed=10 * w.size, transcendentals=0),
        name="split_taps",
    )(w)


def dense_kernel(in_ref, mid_ref, out_ref, hi_ref, lo_ref):
    first = 0
    for ref in (in_ref, mid_ref, out_ref):
        part = slice(first, first + ref.shape[0])
        hi_ref[part, :], lo_ref[part, :] = halves(ref[...])
        first += ref.shape[0]


def split_dense(arrays, parts=2):
    width = arrays[0].shape[1]
    heights = [a.shape[0] // SECTIONS for a in arrays]
    specs = [pl.BlockSpec((h, width // parts), lambda s, c: (s, c)) for h in heights + [sum(heights)] * 2]
    size = sum(a.size for a in arrays)
    return pl.pallas_call(
        dense_kernel,
        grid=(SECTIONS, parts),
        in_specs=specs[:-2],
        out_specs=specs[-2:],
        out_shape=[jax.ShapeDtypeStruct((SECTIONS * sum(heights), width), BF16)] * 2,
        compiler_params=PARAMS,
        cost_estimate=pl.CostEstimate(flops=4 * size, bytes_accessed=8 * size, transcendentals=0),
        name="split_dense",
    )(*arrays)


def dot3(a, w):
    dot = functools.partial(jnp.dot, preferred_element_type=F32)
    return dot(a[0], w[0]) + dot(a[0], w[1]) + dot(a[1], w[0])


def network_kernel(x_ref, cb_ref, tb_ref, *refs):
    n = 4
    sources, h_ref = refs[:n], refs[n]
    held, sems = refs[n + 1 : 2 * n + 1], refs[2 * n + 1]
    rows, width = h_ref.shape
    frames = rows // MICS
    half = TILE // 2

    def fetch(j, k):
        size = width if j < 2 else held[j].shape[0] // SECTIONS
        part = pl.ds(pl.multiple_of(k * size, size), size)
        return pltpu.make_async_copy(sources[j].at[part, :], held[j].at[part, :], sems.at[j, k])

    for s in range(SECTIONS):
        for k in range(3 * LAYERS * s, 3 * LAYERS * (s + 1)):
            for j in range(2):
                fetch(j, k).start()
        for j in range(2, n):
            fetch(j, s).start()

    def weight(j, k):
        part = pl.ds(pl.multiple_of(k * width, width), width)
        return held[j][part, :], held[j + 1][part, :]

    top = lax.broadcasted_iota(jnp.int32, (rows // TILE // 2, TILE, width), 1) < half

    def swap(a):
        return pltpu.roll(a, half, axis=1)

    def pair(h, l):
        if l == 0:
            tiles = h.reshape(rows // TILE // 2, 2, TILE, width)
            a, b = tiles[:, 0], tiles[:, 1]
            even, odd = jnp.where(top, a, swap(b)), jnp.where(top, swap(a), b)
            turned = swap(odd).reshape(MICS, -1, TILE, width)
            before = jnp.concatenate([jnp.zeros((MICS, 1, TILE, width), F32), turned[:, :-1]], axis=1)
            past = jnp.where(top, before.reshape(odd.shape), turned.reshape(odd.shape))
        else:
            groups = h.reshape(MICS, -1, 2, half * 2**l, width)
            even, odd = groups[:, :, 0], groups[:, :, 1]
            past = jnp.concatenate([jnp.zeros_like(odd[:, :1]), odd[:, :-1]], axis=1)
        return [p.reshape(rows // 2, width) for p in (even, odd, past)]

    def join(even, odd, l):
        if l == 0:
            even, odd = (p.reshape(rows // TILE // 2, 1, TILE, width) for p in (even, odd))
            even, odd = even[:, 0], odd[:, 0]
            a, b = jnp.where(top, even, swap(odd)), jnp.where(top, swap(even), odd)
            both = jnp.concatenate([a[:, None], b[:, None]], axis=1)
        else:
            even, odd = (p.reshape(MICS, -1, 1, half * 2**l, width) for p in (even, odd))
            both = jnp.concatenate([even, odd], axis=2)
        return both.reshape(rows, width)

    def layer(h, s, l, eager):
        k = 3 * (s * LAYERS + l)

        def ready(*taps):
            for t in taps:
                for j in range(2):
                    fetch(j, k + t).wait()

        if not eager:
            ready(0, 1, 2)
        even, odd, past = pair(h, l)
        if eager:
            ready(0)
        shared = dot3(halves(even), weight(0, k)) + cb_ref[s, l : l + 1, :]
        if eager:
            ready(1, 2)
        y_odd = shared + dot3(halves(odd - even), weight(0, k + 1))
        y_even = shared + dot3(halves(past - even), weight(0, k + 2))
        h_ref[...] = join(even + jnp.tanh(y_even), odd + jnp.tanh(y_odd), l)

    layer(x_ref[...], 0, 0, True)

    def section(s, _):
        for l in range(1, LAYERS):
            layer(h_ref[...], s, l, False)
        for j in range(2, n):
            fetch(j, s).wait()
        u = jnp.tanh(dot3(halves(h_ref[...]), weight(2, 4 * s)) + tb_ref[s, 0:1, :])
        mixed = dot3(halves(u), weight(2, 4 * s + 2))
        total = u[:frames]
        for m in range(1, MICS):
            total += u[m * frames : (m + 1) * frames]
        v = jnp.tanh(dot3(halves(total * (1.0 / MICS)), weight(2, 4 * s + 1)) + tb_ref[s, 1:2, :])
        pooled = dot3(halves(v), weight(2, 4 * s + 3)) + tb_ref[s, 2:3, :]
        for m in range(MICS):
            part = slice(m * frames, (m + 1) * frames)
            h_ref[part, :] = h_ref[part, :] + jnp.tanh(mixed[part] + pooled)

        @pl.when(s < SECTIONS - 1)
        def _():
            layer(h_ref[...], s + 1, 0, False)

        return 0

    lax.fori_loop(0, SECTIONS, section, 0)


def network(x, biases, weights):
    rows, width = x.shape
    scratch = [pltpu.VMEM(w.shape, w.dtype) for w in weights]
    scratch += [pltpu.SemaphoreType.DMA((len(weights), 3 * SECTIONS * LAYERS))]
    flops = 6 * rows * width * width * SECTIONS * (3 * LAYERS // 2 + 2)
    return pl.pallas_call(
        network_kernel,
        in_specs=[VMEM] * 3 + [ANY] * len(weights),
        out_specs=VMEM,
        out_shape=jax.ShapeDtypeStruct(x.shape, F32),
        scratch_shapes=scratch,
        compiler_params=pltpu.CompilerParams(vmem_limit_bytes=48 << 20),
        cost_estimate=pl.CostEstimate(
            flops=flops, bytes_accessed=8 * x.size + sum(w.nbytes for w in weights), transcendentals=rows * width * 10
        ),
        name="network",
    )(x, *biases, *weights)


def exchange(pieces):
    return lax.all_to_all(pieces, BOTH, 0, 0, tiled=True)


def body(signal, conv_weight, conv_bias, transform_in, transform_mid, transform_out, transform_offsets_bias):
    frames, width = signal.shape[1:]
    devices = lax.axis_size(BOTH)
    held = frames // devices
    pieces = signal.reshape(held, devices, width).transpose(1, 0, 2)
    pieces = exchange(pieces)
    flat = [w.reshape(-1, width) for w in (transform_in, transform_mid, transform_out)]
    weights = [*split_taps(conv_weight.reshape(-1, width)), *split_dense(flat)]
    y = network(pieces.reshape(frames, width), (conv_bias, transform_offsets_bias), weights)
    pieces = exchange(y.reshape(devices, held, width))
    return pieces.transpose(1, 0, 2).reshape(signal.shape)


def solution(mesh):
    placed = (P("mic", "tm", None), P(), P(), P(), P(), P(), P())
    return jax.shard_map(body, mesh=mesh, in_specs=placed, out_specs=P("mic", "tm", None), check_vma=False)
```
